32 devices in a mesh: row: 8 (over y, x, core), col: 4 (over z).
Axes of the slice: x: 2, y: 2, z: 4, core: 2. Of those that a mesh axis runs over, the one named last changes fastest.
Arguments:
- out_grad: bfloat16 [640, 8192], P('col', 'row'), may hold values from -32 to 32
- gate_act: bfloat16 [640, 29568], P('row', 'col'), may hold values from -8 to 8
- up_act: bfloat16 [640, 29568], P('row', 'col'), may hold values from -6 to 6
- gate_codes: int32 [29568, 4096], P('col', 'row'), may hold values from 0 to 255
- gate_scales: int32 [512, 29568], P('row', 'col'), may hold values from 40 to 71
- up_codes: int32 [29568, 4096], P('col', 'row'), may hold values from 0 to 255
- up_scales: int32 [512, 29568], P('row', 'col'), may hold values from 40 to 71
- down_codes: int32 [8192, 14784], P('row', 'col'), may hold values from 0 to 255
- down_scales: int32 [1848, 8192], P('col', 'row'), may hold values from 40 to 71
- tensor_scales: float32 [3], replicated, may hold values from 0.001 to 0.003
Outputs:
- grad_unit: bfloat16 [640, 8192], P('col', 'row')
- grad_amax: float32 [1], replicated
The draws below stay inside these ranges and needn't reach their ends.
Inputs may be any that keep to these rules, and one draw needn't show every extreme that they name: `gate_codes`: each word holds two FP4 (E2M1) codes as in the reference program. `up_codes`: each word holds two FP4 (E2M1) codes as in the reference program. `down_codes`: each word holds two FP4 (E2M1) codes as in the reference program. `gate_scales`: E4M3 codes as in the reference program. `up_scales`: E4M3 codes as in the reference program. `down_scales`: E4M3 codes as in the reference program.
All inputs are finite; a program needn't handle non-finite values. Where the reference program divides by a largest or mean magnitude, that divisor is 1e-20 or more.
Results may differ from the reference program's by a relative error of at most 0.025.
Values may be sent and summed in bfloat16 or wider, within the bound.
A program may use at most 320 MiB of HBM per device.

```python
import math
import jax
import jax.numpy as jnp
from jax import lax

D = 8192
FF = 29568
BLOCK = 16
TOKENS = 640
N_ROW = 8
N_COL = 4


def draw_out_grad(key, part):
    key_noise = jax.random.fold_in(key, 11)
    key_scale = jax.random.fold_in(key, 23)
    positions = jnp.arange(TOKENS, dtype=jnp.float32) / TOKENS
    ramp = jnp.exp(jnp.log(3.0) * positions)
    noise = jax.random.normal(key_noise, (TOKENS, D), jnp.float32)
    token_scale = jnp.exp(jax.random.uniform(key_scale, (TOKENS, 1), jnp.float32, jnp.log(0.3), jnp.log(3.0)))
    return jnp.clip(noise * token_scale * ramp[:, None], -32.0, 32.0).astype(jnp.bfloat16)


def plant(entries, key, low, top_value):
    longest = entries.shape.index(max(entries.shape))
    spots = []
    for shift in (0, 1):
        where = [jax.random.randint(jax.random.fold_in(key, axis), (), 0, length) for axis, length in enumerate(entries.shape)]
        where[longest] = (where[longest] + shift) % entries.shape[longest]
        spots.append(tuple(where))
    return entries.at[spots[0]].set(low).at[spots[1]].set(top_value)


def shard_levels(stream_key, shape, pieces, smallest, top_value):
    factor_of = 1.0
    for axis_at, shards_of in pieces:
        steps = jax.random.uniform(jax.random.fold_in(jax.random.fold_in(stream_key, 6), axis_at), (shards_of,), jnp.float32, smallest / len(pieces), top_value / len(pieces))
        factor_of = factor_of * jnp.repeat(jnp.exp(steps), shape[axis_at] // shards_of).reshape((-1,) + (1,) * (len(shape) - 1 - axis_at))
    return factor_of


def gaussian(stream_key, dims, deviation, most, cuts=(), kind=jnp.bfloat16):
    loudness = shard_levels(stream_key, dims, cuts, -0.22, 0.18) if cuts else 1.0
    drawn = jax.random.normal(stream_key, dims, jnp.float32) * deviation * loudness
    return jnp.minimum(jnp.maximum(drawn, -most), most).astype(kind)


def setup_inputs(seed: int = 0) -> dict:
    seeds = jax.random.split(jax.random.key(seed), 11)
    return {
        "out_grad": draw_out_grad(jax.random.fold_in(seeds[10], 71), 0),
        "gate_act": gaussian(seeds[1], (TOKENS, FF), 2.0, 8.0, ((0, 8), (1, 4))),
        "up_act": gaussian(seeds[2], (TOKENS, FF), 1.0, 6.0, ((0, 8), (1, 4))),
        "gate_codes": plant(jax.random.randint(seeds[3], (FF, D // 2), 0, 256), jax.random.fold_in(seeds[3], 1), 0, 255).astype(jnp.int32),
        "gate_scales": plant(jax.random.randint(seeds[4], (D // BLOCK, FF), 40, 72), jax.random.fold_in(seeds[4], 1), 40, 71).astype(jnp.int32),
        "up_codes": plant(jax.random.randint(seeds[5], (FF, D // 2), 0, 256), jax.random.fold_in(seeds[5], 1), 0, 255).astype(jnp.int32),
        "up_scales": plant(jax.random.randint(seeds[6], (D // BLOCK, FF), 40, 72), jax.random.fold_in(seeds[6], 1), 40, 71).astype(jnp.int32),
        "down_codes": plant(jax.random.randint(seeds[7], (D, FF // 2), 0, 256), jax.random.fold_in(seeds[7], 1), 0, 255).astype(jnp.int32),
        "down_scales": plant(jax.random.randint(seeds[8], (FF // BLOCK, D), 40, 72), jax.random.fold_in(seeds[8], 1), 40, 71).astype(jnp.int32),
        "tensor_scales": jnp.clip(jnp.exp(jax.random.uniform(seeds[9], (3,), jnp.float32, math.log(0.001), math.log(0.003))), 0.001, 0.003),
    }


def fp4_values(packed):
    low_bits = jnp.bitwise_and(packed, 15)
    high_bits = jnp.bitwise_and(jnp.right_shift(packed, 4), 15)
    codes = jnp.stack([low_bits, high_bits], axis=-1).reshape(packed.shape[0], 2 * packed.shape[1])
    magnitude = jnp.bitwise_and(codes, 7).astype(jnp.float32)
    negative = jnp.right_shift(codes, 3).astype(jnp.float32)
    level = jnp.where(magnitude < 4.0, 0.5 * magnitude, jnp.where(magnitude < 6.0, magnitude - 2.0, 2.0 * magnitude - 8.0))
    return level * (1.0 - 2.0 * negative)


def e4m3_values(scale_codes):
    exponent = jnp.right_shift(scale_codes, 3)
    mantissa = jnp.bitwise_and(scale_codes, 7)
    power = jnp.left_shift(jnp.ones_like(exponent), exponent)
    normal_part = ((8 + mantissa) * power).astype(jnp.float32) / 1024.0
    subnormal = mantissa.astype(jnp.float32) / 512.0
    return jnp.where(exponent > 0, normal_part, subnormal)


def dequantize(packed, scale_codes):
    level = fp4_values(packed)
    row_total = level.shape[0]
    col_total = level.shape[1]
    block_scale = e4m3_values(scale_codes).T
    scaled = level.reshape(row_total, block_scale.shape[1], BLOCK) * block_scale[:, :, None]
    return scaled.reshape(row_total, col_total).astype(jnp.bfloat16)


def rounded(value):
    return lax.optimization_barrier(value.astype(jnp.bfloat16)).astype(jnp.float32)


def product(left, right):
    return jnp.dot(left.astype(jnp.float32), right.astype(jnp.float32), precision=lax.Precision.HIGHEST, preferred_element_type=jnp.float32)


def reference(out_grad, gate_act, up_act, gate_codes, gate_scales, up_codes, up_scales, down_codes, down_scales, tensor_scales):
    width_rows = D // N_ROW
    hidden_cols = FF // N_COL

    def down_step(total, block_index):
        first_row = (block_index * width_rows).astype(jnp.int32)
        weight = dequantize(lax.dynamic_slice_in_dim(down_codes, first_row, width_rows, 0),
                            lax.dynamic_slice_in_dim(down_scales, first_row, width_rows, 1))
        grads = lax.dynamic_slice_in_dim(out_grad, first_row, width_rows, 1)
        return total + rounded(product(grads, weight)), None

    hidden_sum, unused = lax.scan(down_step, jnp.zeros((TOKENS, FF), jnp.float32), jnp.arange(N_ROW, dtype=jnp.int32))
    hidden_grad = hidden_sum * tensor_scales[2]
    gate_value = gate_act.astype(jnp.float32)
    up_value = up_act.astype(jnp.float32)
    sigmoid_gate = jax.nn.sigmoid(gate_value)
    gate_grad = (hidden_grad * up_value * sigmoid_gate * (1.0 + gate_value * (1.0 - sigmoid_gate))).astype(jnp.bfloat16)
    up_grad = (hidden_grad * gate_value * sigmoid_gate).astype(jnp.bfloat16)

    def hidden_step(total, block_index):
        first_col = (block_index * hidden_cols).astype(jnp.int32)
        weight_gate = dequantize(lax.dynamic_slice_in_dim(gate_codes, first_col, hidden_cols, 0),
                                 lax.dynamic_slice_in_dim(gate_scales, first_col, hidden_cols, 1))
        weight_up = dequantize(lax.dynamic_slice_in_dim(up_codes, first_col, hidden_cols, 0),
                               lax.dynamic_slice_in_dim(up_scales, first_col, hidden_cols, 1))
        term = tensor_scales[0] * product(lax.dynamic_slice_in_dim(gate_grad, first_col, hidden_cols, 1), weight_gate)
        term = term + tensor_scales[1] * product(lax.dynamic_slice_in_dim(up_grad, first_col, hidden_cols, 1), weight_up)
        return total + rounded(term), None

    width_grad, unused = lax.scan(hidden_step, jnp.zeros((TOKENS, D), jnp.float32), jnp.arange(N_COL, dtype=jnp.int32))
    largest = jnp.max(jnp.abs(width_grad))
    grad_unit = (6.0 * width_grad / (largest + 1e-6)).astype(jnp.bfloat16)
    return grad_unit, largest.reshape(1)
```

```python
import functools

import jax
import jax.numpy as jnp
from jax import lax
from jax.experimental import pallas as pl
from jax.experimental.pallas import tpu as pltpu
from jax.sharding import PartitionSpec as P

BLOCK = 16
GROUP = 128
MESH = pl.DeviceIdType.MESH
F32 = jnp.float32
BF16 = jnp.bfloat16


def half_scales(codes):
    exponent = jnp.right_shift(codes, 3)
    mantissa = jnp.bitwise_and(codes, 7)
    units = jnp.where(exponent > 0, jnp.left_shift(8 + mantissa, exponent), 2 * mantissa)
    return (units.astype(F32) * (1.0 / 2048.0)).astype(BF16)


def double_levels(code):
    x = code.astype(F32).astype(BF16)
    negative = x >= 8.0
    m = jnp.where(negative, x - 8.0, x)
    m2 = m + m
    level = jnp.maximum(jnp.maximum(m, m2 - 4.0), m2 + m2 - 16.0)
    return jnp.where(negative, -level, level)


def spread(scales, words):
    blocks = scales.shape[0]
    row = lax.broadcasted_iota(jnp.int32, (blocks, words), 0)
    col = lax.broadcasted_iota(jnp.int32, (blocks, words), 1)
    one_hot = jnp.where(row == jnp.right_shift(col, 3), 1.0, 0.0).astype(BF16)
    return lax.dot_general(
        scales, one_hot, (((0,), (0,)), ((), ())), preferred_element_type=F32
    ).astype(BF16)


def decode(words, scales):
    s = spread(scales, words.shape[1])
    low = double_levels(jnp.bitwise_and(words, 15)) * s
    high = double_levels(jnp.bitwise_and(jnp.right_shift(words, 4), 15)) * s
    return low, high


def split_order(n):
    row = lax.broadcasted_iota(jnp.int32, (n, n), 0)
    col = lax.broadcasted_iota(jnp.int32, (n, n), 1)
    source = jnp.where(col < n // 2, 2 * col, 2 * (col - n // 2) + 1)
    return jnp.where(row == source, 1.0, 0.0).astype(BF16)


def join_order(n):
    row = lax.broadcasted_iota(jnp.int32, (n, n), 0)
    col = lax.broadcasted_iota(jnp.int32, (n, n), 1)
    target = jnp.where(row < n // 2, 2 * row, 2 * (row - n // 2) + 1)
    return jnp.where(col == target, 1.0, 0.0).astype(BF16)


def down_kernel(grad_ref, codes_ref, scale_ref, out_ref):
    low, high = decode(codes_ref[...], scale_ref[...])
    grads = grad_ref[...]
    out_ref[:, :GROUP] = jnp.dot(grads, low, preferred_element_type=F32).astype(BF16)
    out_ref[:, GROUP:] = jnp.dot(grads, high, preferred_element_type=F32).astype(BF16)


def down(grads, codes, scales, groups):
    tokens, width = grads.shape
    return pl.pallas_call(
        down_kernel,
        out_shape=jax.ShapeDtypeStruct((tokens, groups * 2 * GROUP), BF16),
        grid=(groups,),
        in_specs=[
            pl.BlockSpec((tokens, width), lambda i: (0, 0)),
            pl.BlockSpec((width, GROUP), lambda i: (0, i)),
            pl.BlockSpec((GROUP // 8, width), lambda i: (i, 0)),
        ],
        out_specs=pl.BlockSpec((tokens, 2 * GROUP), lambda i: (0, i)),
        compiler_params=pltpu.CompilerParams(vmem_limit_bytes=40 << 20),
        cost_estimate=pl.CostEstimate(
            flops=4 * tokens * width * groups * GROUP,
            bytes_accessed=4 * width * groups * GROUP,
            transcendentals=0,
        ),
    )(grads, codes, scales)


def act_kernel(hidden_units, ts_ref, hidden_ref, gate_ref, up_ref, gg_ref, ug_ref):
    span = 2 * GROUP
    col = lax.broadcasted_iota(jnp.int32, gate_ref.shape, 1) + pl.program_id(0) * span
    inside = col < hidden_units
    to_split, to_natural = split_order(span), join_order(span)
    zero = jnp.zeros(gate_ref.shape, F32)
    gate_in = jnp.where(inside, gate_ref[...].astype(F32), zero).astype(BF16)
    up_in = jnp.where(inside, up_ref[...].astype(F32), zero).astype(BF16)
    g = jnp.dot(gate_in, to_split, preferred_element_type=F32)
    u = jnp.dot(up_in, to_split, preferred_element_type=F32)
    h = hidden_ref[...].astype(F32) * ts_ref[2]
    sig = jax.nn.sigmoid(g)
    gg = (h * u * sig * (1.0 + g * (1.0 - sig))).astype(BF16)
    ug = (h * g * sig).astype(BF16)
    gg_ref[...] = jnp.dot(gg, to_natural, preferred_element_type=F32).astype(BF16)
    ug_ref[...] = jnp.dot(ug, to_natural, preferred_element_type=F32).astype(BF16)


def act(ts, hidden, gate_rows, up_rows):
    rows, padded = hidden.shape
    span = 2 * GROUP
    block = pl.BlockSpec((rows, span), lambda i: (0, i))
    return pl.pallas_call(
        functools.partial(act_kernel, gate_rows.shape[1]),
        out_shape=[jax.ShapeDtypeStruct((rows, padded), BF16)] * 2,
        grid=(padded // span,),
        in_specs=[pl.BlockSpec(memory_space=pltpu.SMEM), block, block, block],
        out_specs=[block, block],
        compiler_params=pltpu.CompilerParams(vmem_limit_bytes=40 << 20),
    )(ts, hidden, gate_rows, up_rows)


def width_kernel(ts_ref, gg_ref, ug_ref, gc_ref, gs_ref, uc_ref, us_ref, out_ref, acc_g, acc_u):
    step = pl.program_id(0)
    half = gc_ref.shape[1]

    @pl.when(step == 0)
    def _():
        acc_g[...] = jnp.zeros_like(acc_g)
        acc_u[...] = jnp.zeros_like(acc_u)

    for grad_ref, code_ref, scale_ref, acc in (
        (gg_ref, gc_ref, gs_ref, acc_g),
        (ug_ref, uc_ref, us_ref, acc_u),
    ):
        low, high = decode(code_ref[...], scale_ref[...])
        grads = grad_ref[...]
        acc[:, :half] += jnp.dot(grads, low, preferred_element_type=F32)
        acc[:, half:] += jnp.dot(grads, high, preferred_element_type=F32)

    @pl.when(step == pl.num_programs(0) - 1)
    def _():
        out_ref[...] = (ts_ref[0] * acc_g[...] + ts_ref[1] * acc_u[...]).astype(BF16)


def width(ts, gg, ug, gate_codes, gate_scales, up_codes, up_scales):
    tokens, padded = gg.shape
    half = gate_codes.shape[1]
    span = 2 * GROUP
    grads = pl.BlockSpec((tokens, span), lambda i: (0, i))
    codes = pl.BlockSpec((span, half), lambda i: (i, 0))
    scales = pl.BlockSpec((half // 8, span), lambda i: (0, i))
    return pl.pallas_call(
        width_kernel,
        out_shape=jax.ShapeDtypeStruct((tokens, 2 * half), BF16),
        grid=(padded // span,),
        in_specs=[
            pl.BlockSpec(memory_space=pltpu.SMEM), grads, grads, codes, scales, codes, scales,
        ],
        out_specs=pl.BlockSpec((tokens, 2 * half), lambda i: (0, 0)),
        scratch_shapes=[pltpu.VMEM((tokens, 2 * half), F32)] * 2,
        compiler_params=pltpu.CompilerParams(vmem_limit_bytes=48 << 20),
    )(ts, gg, ug, gate_codes, gate_scales, up_codes, up_scales)


def finish_kernel(n_row, n_col, q_ref, unit_ref, amax_ref, recv, total, mine, maxes,
                  send, got, max_send, max_got):
    row, col = lax.axis_index("row"), lax.axis_index("col")
    block = total.shape[0]
    col_peers = [(row, lax.rem(col + d, n_col)) for d in range(1, n_col)]
    row_peers = [(lax.rem(row + d, n_row), col) for d in range(1, n_row)]
    barrier = pltpu.get_barrier_semaphore()
    for peer in col_peers + row_peers:
        pl.semaphore_signal(barrier, inc=1, device_id=peer, device_id_type=MESH)
    pl.semaphore_wait(barrier, n_col + n_row - 2)

    copies = []
    for d, peer in enumerate(col_peers):
        start = pl.multiple_of(peer[1] * block, 16)
        copies.append(pltpu.make_async_remote_copy(
            src_ref=q_ref.at[pl.ds(start, block), :], dst_ref=recv.at[d],
            send_sem=send.at[d], recv_sem=got.at[d], device_id=peer, device_id_type=MESH))
    for copy in copies:
        copy.start()
    total[...] = q_ref[pl.ds(pl.multiple_of(col * block, 16), block), :].astype(F32)
    for d, copy in enumerate(copies):
        copy.wait_recv()
        total[...] += recv[d].astype(F32)
    largest = jnp.max(jnp.abs(total[...]))
    mine[0] = jnp.full(mine.shape[1:], largest, F32)

    def exchange(peers, stage, base):
        out = [pltpu.make_async_remote_copy(
            src_ref=mine.at[stage], dst_ref=maxes.at[base + d], send_sem=max_send.at[base + d],
            recv_sem=max_got.at[base + d], device_id=peer, device_id_type=MESH)
            for d, peer in enumerate(peers)]
        for copy in out:
            copy.start()
        value = mine[stage]
        for d, copy in enumerate(out):
            copy.wait_recv()
            value = jnp.maximum(value, maxes[base + d])
        return out, value

    first, value = exchange(col_peers, 0, 0)
    mine[1] = value
    second, value = exchange(row_peers, 1, n_col - 1)
    amax_ref[...] = value
    unit = (6.0 * total[...] / (value[0:1, 0:1] + 1e-6)).astype(BF16)
    unit_ref[...] = jnp.dot(
        unit, join_order(unit.shape[1]), preferred_element_type=F32).astype(BF16)
    for copy in copies + first + second:
        copy.wait_send()


def finish(q, n_row, n_col):
    tokens, width_here = q.shape
    block = tokens // n_col
    peers = n_row + n_col - 2
    vmem = pl.BlockSpec(memory_space=pltpu.VMEM)
    return pl.pallas_call(
        functools.partial(finish_kernel, n_row, n_col),
        out_shape=[
            jax.ShapeDtypeStruct((block, width_here), BF16),
            jax.ShapeDtypeStruct((8, 128), F32),
        ],
        in_specs=[vmem],
        out_specs=[vmem, vmem],
        scratch_shapes=[
            pltpu.VMEM((n_col - 1, block, width_here), BF16),
            pltpu.VMEM((block, width_here), F32),
            pltpu.VMEM((2, 8, 128), F32),
            pltpu.VMEM((peers, 8, 128), F32),
            pltpu.SemaphoreType.DMA((n_col - 1,)),
            pltpu.SemaphoreType.DMA((n_col - 1,)),
            pltpu.SemaphoreType.DMA((peers,)),
            pltpu.SemaphoreType.DMA((peers,)),
        ],
        compiler_params=pltpu.CompilerParams(
            collective_id=3, has_side_effects=True, vmem_limit_bytes=40 << 20),
    )(q)


def per_device(n_row, n_col, out_grad, gate_act, up_act, gate_codes, gate_scales, up_codes,
               up_scales, down_codes, down_scales, ts):
    groups = pl.cdiv(down_codes.shape[1], GROUP)
    extra = groups * GROUP // 8 - down_scales.shape[0]
    ds = jnp.pad(half_scales(down_scales), ((0, extra), (0, 0)))
    more = groups * 2 * GROUP - gate_scales.shape[1]
    gs = jnp.pad(half_scales(gate_scales), ((0, 0), (0, more)))
    us = jnp.pad(half_scales(up_scales), ((0, 0), (0, more)))
    grads = lax.all_gather(out_grad, "col", axis=0, tiled=True)
    partial = down(grads, down_codes, ds, groups)
    hidden = lax.psum_scatter(partial, "row", scatter_dimension=0, tiled=True)
    gg, ug = act(ts, hidden, gate_act, up_act)
    gg = lax.all_gather(gg, "row", axis=0, tiled=True)
    ug = lax.all_gather(ug, "row", axis=0, tiled=True)
    q = width(ts, gg, ug, gate_codes, gs, up_codes, us)
    unit, amax = finish(q, n_row, n_col)
    return unit, amax[0, 0:1]


def solution(mesh):
    n_row, n_col = mesh.shape["row"], mesh.shape["col"]
    in_specs = (
        P("col", "row"), P("row", "col"), P("row", "col"), P("col", "row"), P("row", "col"),
        P("col", "row"), P("row", "col"), P("row", "col"), P("col", "row"), P(),
    )
    return jax.shard_map(
        functools.partial(per_device, n_row, n_col), mesh=mesh, in_specs=in_specs,
        out_specs=(P("col", "row"), P()), check_vma=False,
    )
```

```python
import functools

import jax
import jax.numpy as jnp
from jax import lax
from jax.experimental import pallas as pl
from jax.experimental.pallas import tpu as pltpu
from jax.sharding import PartitionSpec as P

BLOCK = 16
SPAN = 512
GROUP = 128
MESH = pl.DeviceIdType.MESH
F32 = jnp.float32
BF16 = jnp.bfloat16


def half_scales(codes):
    exponent = jnp.right_shift(codes, 3)
    mantissa = jnp.bitwise_and(codes, 7)
    units = jnp.where(exponent > 0, jnp.left_shift(8 + mantissa, exponent), 2 * mantissa)
    return (units.astype(F32) * (1.0 / 2048.0)).astype(BF16)


def double_levels(code):
    x = code.astype(F32).astype(BF16)
    negative = x >= 8.0
    m = jnp.where(negative, x - 8.0, x)
    m2 = m + m
    level = jnp.maximum(jnp.maximum(m, m2 - 4.0), m2 + m2 - 16.0)
    return jnp.where(negative, -level, level)


def spread(scales, words):
    blocks = scales.shape[0]
    row = lax.broadcasted_iota(jnp.int32, (blocks, words), 0)
    col = lax.broadcasted_iota(jnp.int32, (blocks, words), 1)
    one_hot = jnp.where(row == jnp.right_shift(col, 3), 1.0, 0.0).astype(BF16)
    return lax.dot_general(
        scales, one_hot, (((0,), (0,)), ((), ())), preferred_element_type=F32
    ).astype(BF16)


def decode(words, scales):
    s = spread(scales, words.shape[1])
    low = double_levels(jnp.bitwise_and(words, 15)) * s
    high = double_levels(jnp.bitwise_and(jnp.right_shift(words, 4), 15)) * s
    return low, high


def split_order(n):
    row = lax.broadcasted_iota(jnp.int32, (n, n), 0)
    col = lax.broadcasted_iota(jnp.int32, (n, n), 1)
    source = jnp.where(col < n // 2, 2 * col, 2 * (col - n // 2) + 1)
    return jnp.where(row == source, 1.0, 0.0).astype(BF16)


def join_order(n):
    row = lax.broadcasted_iota(jnp.int32, (n, n), 0)
    col = lax.broadcasted_iota(jnp.int32, (n, n), 1)
    target = jnp.where(row < n // 2, 2 * row, 2 * (row - n // 2) + 1)
    return jnp.where(col == target, 1.0, 0.0).astype(BF16)


def down_kernel(grad_ref, codes_ref, scale_ref, out_ref):
    low, high = decode(codes_ref[...], scale_ref[...])
    grads = grad_ref[...]
    out_ref[:, :GROUP] = jnp.dot(grads, low, preferred_element_type=F32).astype(BF16)
    out_ref[:, GROUP:] = jnp.dot(grads, high, preferred_element_type=F32).astype(BF16)


def down(grads, codes, scales, groups):
    tokens, width = grads.shape
    return pl.pallas_call(
        down_kernel,
        out_shape=jax.ShapeDtypeStruct((tokens, groups * 2 * GROUP), BF16),
        grid=(groups,),
        in_specs=[
            pl.BlockSpec((tokens, width), lambda i: (0, 0)),
            pl.BlockSpec((width, GROUP), lambda i: (0, i)),
            pl.BlockSpec((GROUP // 8, width), lambda i: (i, 0)),
        ],
        out_specs=pl.BlockSpec((tokens, 2 * GROUP), lambda i: (0, i)),
        compiler_params=pltpu.CompilerParams(vmem_limit_bytes=40 << 20),
        cost_estimate=pl.CostEstimate(
            flops=4 * tokens * width * groups * GROUP,
            bytes_accessed=4 * width * groups * GROUP,
            transcendentals=0,
        ),
    )(grads, codes, scales)


def act_kernel(hidden_units, ts_ref, hidden_ref, gate_ref, up_ref, out_ref):
    span, unit = gate_ref.shape[1], 2 * GROUP
    to_split, to_natural = split_order(unit), join_order(unit)
    for part in range(span // unit):
        cols = slice(part * unit, (part + 1) * unit)
        shape = (gate_ref.shape[0], unit)
        col = lax.broadcasted_iota(jnp.int32, shape, 1) + pl.program_id(0) * span + part * unit
        inside = col < hidden_units
        zero = jnp.zeros(shape, F32)
        gate_in = jnp.where(inside, gate_ref[:, cols].astype(F32), zero).astype(BF16)
        up_in = jnp.where(inside, up_ref[:, cols].astype(F32), zero).astype(BF16)
        g = jnp.dot(gate_in, to_split, preferred_element_type=F32)
        u = jnp.dot(up_in, to_split, preferred_element_type=F32)
        h = hidden_ref[:, cols].astype(F32) * ts_ref[2]
        sig = jax.nn.sigmoid(g)
        gg = (h * u * sig * (1.0 + g * (1.0 - sig))).astype(BF16)
        ug = (h * g * sig).astype(BF16)
        gg = jnp.dot(gg, to_natural, preferred_element_type=F32)
        ug = jnp.dot(ug, to_natural, preferred_element_type=F32)
        out_ref[0, 0, :, cols] = jnp.where(inside, gg, zero).astype(BF16)
        out_ref[0, 1, :, cols] = jnp.where(inside, ug, zero).astype(BF16)


def act(ts, hidden, gate_rows, up_rows, steps):
    rows = hidden.shape[0]
    block = pl.BlockSpec((rows, SPAN), lambda i: (0, i))
    return pl.pallas_call(
        functools.partial(act_kernel, gate_rows.shape[1]),
        out_shape=jax.ShapeDtypeStruct((steps, 2, rows, SPAN), BF16),
        grid=(steps,),
        in_specs=[pl.BlockSpec(memory_space=pltpu.SMEM), block, block, block],
        out_specs=pl.BlockSpec((1, 2, rows, SPAN), lambda i: (i, 0, 0, 0)),
        compiler_params=pltpu.CompilerParams(vmem_limit_bytes=40 << 20),
    )(ts, hidden, gate_rows, up_rows)


LAG = 2


def width_kernel(n_row, n_col, steps, ts_ref, own_ref, gc_ref, gs_ref, uc_ref, us_ref,
                 unit_ref, amax_ref, held, acc_g, acc_u, q_buf, recv, total, mine, maxes,
                 own_sem, far_send, far_got, hop_send, hop_got, near_send, near_got,
                 send, got, max_send, max_got):
    step = pl.program_id(0)
    half = gc_ref.shape[1]
    row, col = lax.axis_index("row"), lax.axis_index("col")
    chips = n_row // 2
    chip, core = row // 2, lax.rem(row, 2)
    relay = chips == 4
    partner = (chip * 2 + (1 - core), col)
    block = total.shape[0]
    col_peers = [(row, lax.rem(col + d, n_col)) for d in range(1, n_col)]
    row_peers = [(lax.rem(row + d, n_row), col) for d in range(1, n_row)]

    def other(q):
        flipped = chip
        bit = 1
        while bit < chips:
            if q & bit:
                flipped = flipped + bit - 2 * bit * lax.rem(chip // bit, 2)
            bit *= 2
        return flipped

    direct = (1, 2) if relay else tuple(range(1, chips))
    peer_of = {q: (other(q) * 2 + core, col) for q in range(1, chips)}
    row_of = {q: other(q) * 2 + core for q in range(1, chips)}
    row_of[0] = row

    def own_copy(j):
        return pltpu.make_async_copy(own_ref.at[j], held.at[j, row], own_sem.at[j])

    def far_copy(j, q):
        return pltpu.make_async_remote_copy(
            src_ref=own_ref.at[j], dst_ref=held.at[j, row], send_sem=far_send.at[j, q],
            recv_sem=far_got.at[j, q], device_id=peer_of[q], device_id_type=MESH)

    def hop_copy(j, h):
        source, target = (1, 2) if h == 0 else (2, 1)
        return pltpu.make_async_remote_copy(
            src_ref=held.at[j, row_of[source], h], dst_ref=held.at[j, row_of[source], h],
            send_sem=hop_send.at[j, h], recv_sem=hop_got.at[j, h],
            device_id=peer_of[target], device_id_type=MESH)

    def near_copy(j, q):
        src = own_ref.at[j] if q == 0 else held.at[j, row_of[q]]
        return pltpu.make_async_remote_copy(
            src_ref=src, dst_ref=held.at[j, row_of[q]], send_sem=near_send.at[j, q],
            recv_sem=near_got.at[j, q], device_id=partner, device_id_type=MESH)

    @pl.when(step == 0)
    def _():
        barrier = pltpu.get_barrier_semaphore()
        for peer in col_peers + row_peers:
            pl.semaphore_signal(barrier, inc=1, device_id=peer, device_id_type=MESH)
        pl.semaphore_wait(barrier, n_col + n_row - 2)

        @pl.loop(0, steps)
        def _(j):
            for q in direct:
                far_copy(j, q).start()
            near_copy(j, 0).start()
            own_copy(j).start()

        acc_g[...] = jnp.zeros_like(acc_g)
        acc_u[...] = jnp.zeros_like(acc_u)

    @pl.when(step < steps)
    def _():
        for q in direct:
            far_copy(step, q).wait_recv()
            if relay:
                hop_copy(step, q - 1).start()
            near_copy(step, q).start()

    if relay:
        @pl.when(jnp.logical_and(step >= 1, step < steps + 1))
        def _():
            for h in range(2):
                hop_copy(step - 1, h).wait_recv()
            near_copy(step - 1, 3).start()

    @pl.when(step >= LAG)
    def _():
        j = step - LAG
        own_copy(j).wait()
        for q in range(chips):
            near_copy(j, q).wait_recv()
        for part, code_ref, scale_ref, acc in (
            (0, gc_ref, gs_ref, acc_g),
            (1, uc_ref, us_ref, acc_u),
        ):
            low, high = decode(code_ref[...], scale_ref[...])
            grads = held[j, :, part].reshape(acc.shape[0], SPAN)
            acc[:, :half] += jnp.dot(grads, low, preferred_element_type=F32)
            acc[:, half:] += jnp.dot(grads, high, preferred_element_type=F32)

    @pl.when(step == steps + LAG - 1)
    def _():
        q_buf[...] = (ts_ref[0] * acc_g[...] + ts_ref[1] * acc_u[...]).astype(BF16)
        copies = []
        for d, peer in enumerate(col_peers):
            start = pl.multiple_of(peer[1] * block, 16)
            copies.append(pltpu.make_async_remote_copy(
                src_ref=q_buf.at[pl.ds(start, block), :], dst_ref=recv.at[d],
                send_sem=send.at[d], recv_sem=got.at[d], device_id=peer, device_id_type=MESH))
        for copy in copies:
            copy.start()
        total[...] = q_buf[pl.ds(pl.multiple_of(col * block, 16), block), :].astype(F32)
        for d, copy in enumerate(copies):
            copy.wait_recv()
            total[...] += recv[d].astype(F32)
        largest = jnp.max(jnp.abs(total[...]))
        mine[0] = jnp.full(mine.shape[1:], largest, F32)

        def exchange(peers, stage, base):
            out = [pltpu.make_async_remote_copy(
                src_ref=mine.at[stage], dst_ref=maxes.at[base + d],
                send_sem=max_send.at[base + d], recv_sem=max_got.at[base + d],
                device_id=peer, device_id_type=MESH) for d, peer in enumerate(peers)]
            for copy in out:
                copy.start()
            value = mine[stage]
            for d, copy in enumerate(out):
                copy.wait_recv()
                value = jnp.maximum(value, maxes[base + d])
            return out, value

        first, value = exchange(col_peers, 0, 0)
        mine[1] = value
        second, value = exchange(row_peers, 1, n_col - 1)
        amax_ref[...] = value
        unit = (6.0 * total[...] / (value[0:1, 0:1] + 1e-6)).astype(BF16)
        unit_ref[...] = jnp.dot(
            unit, join_order(unit.shape[1]), preferred_element_type=F32).astype(BF16)
        for copy in copies + first + second:
            copy.wait_send()

        @pl.loop(0, steps)
        def _(j):
            for q in direct:
                far_copy(j, q).wait_send()
                if relay:
                    hop_copy(j, q - 1).wait_send()
            for q in range(chips):
                near_copy(j, q).wait_send()


def width(ts, own, gate_codes, gate_scales, up_codes, up_scales, n_row, n_col):
    steps, _, rows, _ = own.shape
    half = gate_codes.shape[1]
    tokens, chips, peers = rows * n_row, n_row // 2, n_row + n_col - 2
    block = tokens // n_col
    codes = pl.BlockSpec((SPAN, half), lambda i: (jnp.maximum(i - LAG, 0), 0))
    scales = pl.BlockSpec((half // 8, SPAN), lambda i: (0, jnp.maximum(i - LAG, 0)))
    dma = pltpu.SemaphoreType.DMA
    return pl.pallas_call(
        functools.partial(width_kernel, n_row, n_col, steps),
        out_shape=[
            jax.ShapeDtypeStruct((block, 2 * half), BF16),
            jax.ShapeDtypeStruct((8, 128), F32),
        ],
        grid=(steps + LAG,),
        in_specs=[
            pl.BlockSpec(memory_space=pltpu.SMEM), pl.BlockSpec(memory_space=pl.ANY),
            codes, scales, codes, scales,
        ],
        out_specs=[
            pl.BlockSpec((block, 2 * half), lambda i: (0, 0)),
            pl.BlockSpec((8, 128), lambda i: (0, 0)),
        ],
        scratch_shapes=[
            pltpu.VMEM((steps, n_row, 2, rows, SPAN), BF16),
            pltpu.VMEM((tokens, 2 * half), F32),
            pltpu.VMEM((tokens, 2 * half), F32),
            pltpu.VMEM((tokens, 2 * half), BF16),
            pltpu.VMEM((n_col - 1, block, 2 * half), BF16),
            pltpu.VMEM((block, 2 * half), F32),
            pltpu.VMEM((2, 8, 128), F32),
            pltpu.VMEM((peers, 8, 128), F32),
            dma((steps,)),
            dma((steps, chips)),
            dma((steps, chips)),
            dma((steps, 2)),
            dma((steps, 2)),
            dma((steps, chips)),
            dma((steps, chips)),
            dma((n_col - 1,)),
            dma((n_col - 1,)),
            dma((peers,)),
            dma((peers,)),
        ],
        compiler_params=pltpu.CompilerParams(
            collective_id=3, has_side_effects=True, vmem_limit_bytes=60 << 20,
            dimension_semantics=("arbitrary",)),
    )(ts, own, gate_codes, gate_scales, up_codes, up_scales)


def per_device(n_row, n_col, out_grad, gate_act, up_act, gate_codes, gate_scales, up_codes,
               up_scales, down_codes, down_scales, ts):
    groups = pl.cdiv(down_codes.shape[1], GROUP)
    extra = groups * GROUP // 8 - down_scales.shape[0]
    ds = jnp.pad(half_scales(down_scales), ((0, extra), (0, 0)))
    steps = pl.cdiv(gate_scales.shape[1], SPAN)
    more = steps * SPAN - gate_scales.shape[1]
    gs = jnp.pad(half_scales(gate_scales), ((0, 0), (0, more)))
    us = jnp.pad(half_scales(up_scales), ((0, 0), (0, more)))
    grads = lax.all_gather(out_grad, "col", axis=0, tiled=True)
    partial = down(grads, down_codes, ds, groups)
    hidden = lax.psum_scatter(partial, "row", scatter_dimension=0, tiled=True)
    own = act(ts, hidden, gate_act, up_act, steps)
    unit, amax = width(ts, own, gate_codes, gs, up_codes, us, n_row, n_col)
    return unit, amax[0, 0:1]


def solution(mesh):
    n_row, n_col = mesh.shape["row"], mesh.shape["col"]
    in_specs = (
        P("col", "row"), P("row", "col"), P("row", "col"), P("col", "row"), P("row", "col"),
        P("col", "row"), P("row", "col"), P("row", "col"), P("col", "row"), P(),
    )
    return jax.shard_map(
        functools.partial(per_device, n_row, n_col), mesh=mesh, in_specs=in_specs,
        out_specs=(P("col", "row"), P()), check_vma=False,
    )
```

```python
import functools

import jax
import jax.numpy as jnp
from jax import lax
from jax.experimental import pallas as pl
from jax.experimental.pallas import tpu as pltpu
from jax.sharding import PartitionSpec as P

BLOCK = 16
SPAN = 512
GROUP = 128
MESH = pl.DeviceIdType.MESH
F32 = jnp.float32
BF16 = jnp.bfloat16


def half_scales(codes):
    exponent = jnp.right_shift(codes, 3)
    mantissa = jnp.bitwise_and(codes, 7)
    units = jnp.where(exponent > 0, jnp.left_shift(8 + mantissa, exponent), 2 * mantissa)
    return (units.astype(F32) * (1.0 / 2048.0)).astype(BF16)


def double_levels(code):
    x = code.astype(F32).astype(BF16)
    negative = x >= 8.0
    m = jnp.where(negative, x - 8.0, x)
    m2 = m + m
    level = jnp.maximum(jnp.maximum(m, m2 - 4.0), m2 + m2 - 16.0)
    return jnp.where(negative, -level, level)


def spread(scales, words):
    blocks = scales.shape[0]
    row = lax.broadcasted_iota(jnp.int32, (blocks, words), 0)
    col = lax.broadcasted_iota(jnp.int32, (blocks, words), 1)
    one_hot = jnp.where(row == jnp.right_shift(col, 3), 1.0, 0.0).astype(BF16)
    return lax.dot_general(
        scales, one_hot, (((0,), (0,)), ((), ())), preferred_element_type=F32
    ).astype(BF16)


def decode(words, scales):
    s = spread(scales, words.shape[1])
    low = double_levels(jnp.bitwise_and(words, 15)) * s
    high = double_levels(jnp.bitwise_and(jnp.right_shift(words, 4), 15)) * s
    return low, high


def split_order(n):
    row = lax.broadcasted_iota(jnp.int32, (n, n), 0)
    col = lax.broadcasted_iota(jnp.int32, (n, n), 1)
    source = jnp.where(col < n // 2, 2 * col, 2 * (col - n // 2) + 1)
    return jnp.where(row == source, 1.0, 0.0).astype(BF16)


def join_order(n):
    row = lax.broadcasted_iota(jnp.int32, (n, n), 0)
    col = lax.broadcasted_iota(jnp.int32, (n, n), 1)
    target = jnp.where(row < n // 2, 2 * row, 2 * (row - n // 2) + 1)
    return jnp.where(col == target, 1.0, 0.0).astype(BF16)


def decode_rows(words, scales):
    blocks, wide = scales.shape
    s = jnp.broadcast_to(scales.astype(F32)[:, None, :], (blocks, 8, wide))
    s = s.reshape(blocks * 8, wide).astype(BF16)
    low = double_levels(jnp.bitwise_and(words, 15)) * s
    high = double_levels(jnp.bitwise_and(jnp.right_shift(words, 4), 15)) * s
    return low, high


def flip(chip, q, chips):
    flipped = chip
    bit = 1
    while bit < chips:
        if q & bit:
            flipped = flipped + bit - 2 * bit * lax.rem(chip // bit, 2)
        bit *= 2
    return flipped


DOWN_LAG = 4


def down_kernel(n_row, n_col, groups, own_ref, codes_ref, scale_ref, out_ref, grads, parts,
                near, sums, far, own_sem, all_send, all_got, near_send, near_got, far_send,
                far_got):
    step = pl.program_id(0)
    row, col = lax.axis_index("row"), lax.axis_index("col")
    chips = n_row // 2
    chip, core = row // 2, lax.rem(row, 2)
    partner = (chip * 2 + (1 - core), col)
    rows, span = out_ref.shape
    col_peers = [(row, lax.rem(col + d, n_col)) for d in range(1, n_col)]
    peers = [(flip(chip, q, chips) * 2 + core, col) for q in range(1, chips)]

    def near_copy(j):
        return pltpu.make_async_remote_copy(
            src_ref=parts.at[j, 1 - core], dst_ref=near.at[j], send_sem=near_send.at[j],
            recv_sem=near_got.at[j], device_id=partner, device_id_type=MESH)

    def far_copy(j, q):
        return pltpu.make_async_remote_copy(
            src_ref=sums.at[j, flip(chip, q, chips)], dst_ref=far.at[j, q - 1],
            send_sem=far_send.at[j, q - 1], recv_sem=far_got.at[j, q - 1],
            device_id=peers[q - 1], device_id_type=MESH)

    @pl.when(step == 0)
    def _():
        barrier = pltpu.get_barrier_semaphore()
        for peer in col_peers + peers + [partner]:
            pl.semaphore_signal(barrier, inc=1, device_id=peer, device_id_type=MESH)
        pl.semaphore_wait(barrier, n_col - 1 + chips)
        copies = [pltpu.make_async_remote_copy(
            src_ref=own_ref, dst_ref=grads.at[col], send_sem=all_send.at[d],
            recv_sem=all_got.at[d], device_id=peer, device_id_type=MESH)
            for d, peer in enumerate(col_peers)]
        for copy in copies:
            copy.start()
        mine = pltpu.make_async_copy(own_ref, grads.at[col], own_sem)
        mine.start()
        mine.wait()
        for copy in copies:
            copy.wait()

    @pl.when(step < groups)
    def _():
        low, high = decode_rows(codes_ref[...], scale_ref[...])
        left = grads[...].reshape(n_row * rows, grads.shape[2])
        for h, weight in enumerate((low, high)):
            part = lax.dot_general(
                left, weight, (((1,), (1,)), ((), ())), preferred_element_type=F32
            ).astype(BF16).reshape(chips, 2, rows, GROUP)
            for c in range(2):
                parts[step, c, :, :, h * GROUP:(h + 1) * GROUP] = part[:, c]
        near_copy(step).start()

    @pl.when(jnp.logical_and(step >= 1, step <= groups))
    def _():
        j = step - 1
        near_copy(j).wait_recv()
        sums[j] = (parts[j, core].astype(F32) + near[j].astype(F32)).astype(BF16)
        for q in range(1, chips):
            far_copy(j, q).start()

    @pl.when(step >= DOWN_LAG)
    def _():
        j = step - DOWN_LAG
        value = sums[j, chip].astype(F32)
        for q in range(1, chips):
            far_copy(j, q).wait_recv()
            value = value + far[j, q - 1].astype(F32)
        out_ref[...] = value

    @pl.when(step == groups + DOWN_LAG - 1)
    def _():
        @pl.loop(0, groups)
        def _(j):
            near_copy(j).wait_send()
            for q in range(1, chips):
                far_copy(j, q).wait_send()


def down(out_grad, codes, scales, groups, n_row, n_col):
    here, wide = out_grad.shape
    rows, chips, span = here * n_col // n_row, n_row // 2, 2 * GROUP
    dma = pltpu.SemaphoreType.DMA
    return pl.pallas_call(
        functools.partial(down_kernel, n_row, n_col, groups),
        out_shape=jax.ShapeDtypeStruct((rows, groups * span), F32),
        grid=(groups + DOWN_LAG,),
        in_specs=[
            pl.BlockSpec(memory_space=pl.ANY),
            pl.BlockSpec((GROUP, wide), lambda i: (jnp.minimum(i, groups - 1), 0)),
            pl.BlockSpec((GROUP // 8, wide), lambda i: (jnp.minimum(i, groups - 1), 0)),
        ],
        out_specs=pl.BlockSpec((rows, span), lambda i: (0, jnp.maximum(i - DOWN_LAG, 0))),
        scratch_shapes=[
            pltpu.VMEM((n_col, here, wide), BF16),
            pltpu.VMEM((groups, 2, chips, rows, span), BF16),
            pltpu.VMEM((groups, chips, rows, span), BF16),
            pltpu.VMEM((groups, chips, rows, span), BF16),
            pltpu.VMEM((groups, chips - 1, rows, span), BF16),
            dma,
            dma((n_col - 1,)),
            dma((n_col - 1,)),
            dma((groups,)),
            dma((groups,)),
            dma((groups, chips - 1)),
            dma((groups, chips - 1)),
        ],
        compiler_params=pltpu.CompilerParams(
            collective_id=4, has_side_effects=True, vmem_limit_bytes=60 << 20,
            dimension_semantics=("arbitrary",)),
    )(out_grad, codes, scales)


def act_kernel(hidden_units, ts_ref, hidden_ref, gate_ref, up_ref, out_ref):
    span, unit = gate_ref.shape[1], 2 * GROUP
    to_split, to_natural = split_order(unit), join_order(unit)
    for part in range(span // unit):
        cols = slice(part * unit, (part + 1) * unit)
        shape = (gate_ref.shape[0], unit)
        col = lax.broadcasted_iota(jnp.int32, shape, 1) + pl.program_id(0) * span + part * unit
        inside = col < hidden_units
        zero = jnp.zeros(shape, F32)
        gate_in = jnp.where(inside, gate_ref[:, cols].astype(F32), zero).astype(BF16)
        up_in = jnp.where(inside, up_ref[:, cols].astype(F32), zero).astype(BF16)
        g = jnp.dot(gate_in, to_split, preferred_element_type=F32)
        u = jnp.dot(up_in, to_split, preferred_element_type=F32)
        h = hidden_ref[:, cols].astype(F32) * ts_ref[2]
        sig = jax.nn.sigmoid(g)
        gg = (h * u * sig * (1.0 + g * (1.0 - sig))).astype(BF16)
        ug = (h * g * sig).astype(BF16)
        gg = jnp.dot(gg, to_natural, preferred_element_type=F32)
        ug = jnp.dot(ug, to_natural, preferred_element_type=F32)
        out_ref[0, 0, :, cols] = jnp.where(inside, gg, zero).astype(BF16)
        out_ref[0, 1, :, cols] = jnp.where(inside, ug, zero).astype(BF16)


def act(ts, hidden, gate_rows, up_rows, steps):
    rows = hidden.shape[0]
    block = pl.BlockSpec((rows, SPAN), lambda i: (0, i))
    return pl.pallas_call(
        functools.partial(act_kernel, gate_rows.shape[1]),
        out_shape=jax.ShapeDtypeStruct((steps, 2, rows, SPAN), BF16),
        grid=(steps,),
        in_specs=[pl.BlockSpec(memory_space=pltpu.SMEM), block, block, block],
        out_specs=pl.BlockSpec((1, 2, rows, SPAN), lambda i: (i, 0, 0, 0)),
        compiler_params=pltpu.CompilerParams(vmem_limit_bytes=40 << 20),
    )(ts, hidden, gate_rows, up_rows)


LAG = 2


def width_kernel(n_row, n_col, steps, ts_ref, own_ref, gc_ref, gs_ref, uc_ref, us_ref,
                 unit_ref, amax_ref, held, acc_g, acc_u, q_buf, recv, total, mine, maxes,
                 own_sem, far_send, far_got, hop_send, hop_got, near_send, near_got,
                 send, got, max_send, max_got):
    step = pl.program_id(0)
    half = gc_ref.shape[1]
    row, col = lax.axis_index("row"), lax.axis_index("col")
    chips = n_row // 2
    chip, core = row // 2, lax.rem(row, 2)
    relay = chips == 4
    partner = (chip * 2 + (1 - core), col)
    block = total.shape[0]
    col_peers = [(row, lax.rem(col + d, n_col)) for d in range(1, n_col)]
    row_peers = [(lax.rem(row + d, n_row), col) for d in range(1, n_row)]

    def other(q):
        flipped = chip
        bit = 1
        while bit < chips:
            if q & bit:
                flipped = flipped + bit - 2 * bit * lax.rem(chip // bit, 2)
            bit *= 2
        return flipped

    direct = (1, 2) if relay else tuple(range(1, chips))
    peer_of = {q: (other(q) * 2 + core, col) for q in range(1, chips)}
    row_of = {q: other(q) * 2 + core for q in range(1, chips)}
    row_of[0] = row

    def own_copy(j):
        return pltpu.make_async_copy(own_ref.at[j], held.at[j, row], own_sem.at[j])

    def far_copy(j, q):
        return pltpu.make_async_remote_copy(
            src_ref=own_ref.at[j], dst_ref=held.at[j, row], send_sem=far_send.at[j, q],
            recv_sem=far_got.at[j, q], device_id=peer_of[q], device_id_type=MESH)

    def hop_copy(j, h):
        source, target = (1, 2) if h == 0 else (2, 1)
        return pltpu.make_async_remote_copy(
            src_ref=held.at[j, row_of[source], h], dst_ref=held.at[j, row_of[source], h],
            send_sem=hop_send.at[j, h], recv_sem=hop_got.at[j, h],
            device_id=peer_of[target], device_id_type=MESH)

    def near_copy(j, q):
        src = own_ref.at[j] if q == 0 else held.at[j, row_of[q]]
        return pltpu.make_async_remote_copy(
            src_ref=src, dst_ref=held.at[j, row_of[q]], send_sem=near_send.at[j, q],
            recv_sem=near_got.at[j, q], device_id=partner, device_id_type=MESH)

    @pl.when(step == 0)
    def _():
        barrier = pltpu.get_barrier_semaphore()
        for peer in col_peers + row_peers:
            pl.semaphore_signal(barrier, inc=1, device_id=peer, device_id_type=MESH)
        pl.semaphore_wait(barrier, n_col + n_row - 2)

        @pl.loop(0, steps)
        def _(j):
            for q in direct:
                far_copy(j, q).start()
            near_copy(j, 0).start()
            own_copy(j).start()

        acc_g[...] = jnp.zeros_like(acc_g)
        acc_u[...] = jnp.zeros_like(acc_u)

    @pl.when(step < steps)
    def _():
        for q in direct:
            far_copy(step, q).wait_recv()
            if relay:
                hop_copy(step, q - 1).start()
            near_copy(step, q).start()

    if relay:
        @pl.when(jnp.logical_and(step >= 1, step < steps + 1))
        def _():
            for h in range(2):
                hop_copy(step - 1, h).wait_recv()
            near_copy(step - 1, 3).start()

    @pl.when(step >= LAG)
    def _():
        j = step - LAG
        own_copy(j).wait()
        for q in range(chips):
            near_copy(j, q).wait_recv()
        for part, code_ref, scale_ref, acc in (
            (0, gc_ref, gs_ref, acc_g),
            (1, uc_ref, us_ref, acc_u),
        ):
            low, high = decode(code_ref[...], scale_ref[...])
            grads = held[j, :, part].reshape(acc.shape[0], SPAN)
            acc[:, :half] += jnp.dot(grads, low, preferred_element_type=F32)
            acc[:, half:] += jnp.dot(grads, high, preferred_element_type=F32)

    @pl.when(step == steps + LAG - 1)
    def _():
        q_buf[...] = (ts_ref[0] * acc_g[...] + ts_ref[1] * acc_u[...]).astype(BF16)
        copies = []
        for d, peer in enumerate(col_peers):
            start = pl.multiple_of(peer[1] * block, 16)
            copies.append(pltpu.make_async_remote_copy(
                src_ref=q_buf.at[pl.ds(start, block), :], dst_ref=recv.at[d],
                send_sem=send.at[d], recv_sem=got.at[d], device_id=peer, device_id_type=MESH))
        for copy in copies:
            copy.start()
        total[...] = q_buf[pl.ds(pl.multiple_of(col * block, 16), block), :].astype(F32)
        for d, copy in enumerate(copies):
            copy.wait_recv()
            total[...] += recv[d].astype(F32)
        largest = jnp.max(jnp.abs(total[...]))
        mine[0] = jnp.full(mine.shape[1:], largest, F32)

        def exchange(peers, stage, base):
            out = [pltpu.make_async_remote_copy(
                src_ref=mine.at[stage], dst_ref=maxes.at[base + d],
                send_sem=max_send.at[base + d], recv_sem=max_got.at[base + d],
                device_id=peer, device_id_type=MESH) for d, peer in enumerate(peers)]
            for copy in out:
                copy.start()
            value = mine[stage]
            for d, copy in enumerate(out):
                copy.wait_recv()
                value = jnp.maximum(value, maxes[base + d])
            return out, value

        first, value = exchange(col_peers, 0, 0)
        mine[1] = value
        second, value = exchange(row_peers, 1, n_col - 1)
        amax_ref[...] = value
        unit = (6.0 * total[...] / (value[0:1, 0:1] + 1e-6)).astype(BF16)
        unit_ref[...] = jnp.dot(
            unit, join_order(unit.shape[1]), preferred_element_type=F32).astype(BF16)
        for copy in copies + first + second:
            copy.wait_send()

        @pl.loop(0, steps)
        def _(j):
            for q in direct:
                far_copy(j, q).wait_send()
                if relay:
                    hop_copy(j, q - 1).wait_send()
            for q in range(chips):
                near_copy(j, q).wait_send()


def width(ts, own, gate_codes, gate_scales, up_codes, up_scales, n_row, n_col):
    steps, _, rows, _ = own.shape
    half = gate_codes.shape[1]
    tokens, chips, peers = rows * n_row, n_row // 2, n_row + n_col - 2
    block = tokens // n_col
    codes = pl.BlockSpec((SPAN, half), lambda i: (jnp.maximum(i - LAG, 0), 0))
    scales = pl.BlockSpec((half // 8, SPAN), lambda i: (0, jnp.maximum(i - LAG, 0)))
    dma = pltpu.SemaphoreType.DMA
    return pl.pallas_call(
        functools.partial(width_kernel, n_row, n_col, steps),
        out_shape=[
            jax.ShapeDtypeStruct((block, 2 * half), BF16),
            jax.ShapeDtypeStruct((8, 128), F32),
        ],
        grid=(steps + LAG,),
        in_specs=[
            pl.BlockSpec(memory_space=pltpu.SMEM), pl.BlockSpec(memory_space=pl.ANY),
            codes, scales, codes, scales,
        ],
        out_specs=[
            pl.BlockSpec((block, 2 * half), lambda i: (0, 0)),
            pl.BlockSpec((8, 128), lambda i: (0, 0)),
        ],
        scratch_shapes=[
            pltpu.VMEM((steps, n_row, 2, rows, SPAN), BF16),
            pltpu.VMEM((tokens, 2 * half), F32),
            pltpu.VMEM((tokens, 2 * half), F32),
            pltpu.VMEM((tokens, 2 * half), BF16),
            pltpu.VMEM((n_col - 1, block, 2 * half), BF16),
            pltpu.VMEM((block, 2 * half), F32),
            pltpu.VMEM((2, 8, 128), F32),
            pltpu.VMEM((peers, 8, 128), F32),
            dma((steps,)),
            dma((steps, chips)),
            dma((steps, chips)),
            dma((steps, 2)),
            dma((steps, 2)),
            dma((steps, chips)),
            dma((steps, chips)),
            dma((n_col - 1,)),
            dma((n_col - 1,)),
            dma((peers,)),
            dma((peers,)),
        ],
        compiler_params=pltpu.CompilerParams(
            collective_id=3, has_side_effects=True, vmem_limit_bytes=60 << 20,
            dimension_semantics=("arbitrary",)),
    )(ts, own, gate_codes, gate_scales, up_codes, up_scales)


def per_device(n_row, n_col, out_grad, gate_act, up_act, gate_codes, gate_scales, up_codes,
               up_scales, down_codes, down_scales, ts):
    groups = pl.cdiv(down_codes.shape[1], GROUP)
    extra = groups * GROUP // 8 - down_scales.shape[0]
    ds = jnp.pad(half_scales(down_scales), ((0, extra), (0, 0)))
    steps = pl.cdiv(gate_scales.shape[1], SPAN)
    more = steps * SPAN - gate_scales.shape[1]
    gs = jnp.pad(half_scales(gate_scales), ((0, 0), (0, more)))
    us = jnp.pad(half_scales(up_scales), ((0, 0), (0, more)))
    hidden = down(out_grad, down_codes.T, ds, groups, n_row, n_col)
    own = act(ts, hidden, gate_act, up_act, steps)
    unit, amax = width(ts, own, gate_codes, gs, up_codes, us, n_row, n_col)
    return unit, amax[0, 0:1]


def solution(mesh):
    n_row, n_col = mesh.shape["row"], mesh.shape["col"]
    in_specs = (
        P("col", "row"), P("row", "col"), P("row", "col"), P("col", "row"), P("row", "col"),
        P("col", "row"), P("row", "col"), P("row", "col"), P("col", "row"), P(),
    )
    return jax.shard_map(
        functools.partial(per_device, n_row, n_col), mesh=mesh, in_specs=in_specs,
        out_specs=(P("col", "row"), P()), check_vma=False,
    )
```
